32 devices in a mesh: dp: 2 (over x), row: 4 (over z), col: 4 (over y, core).
Axes of the slice: x: 2, y: 2, z: 4, core: 2. Of those that a mesh axis runs over, the one named last changes fastest.
Arguments:
- layer_input: bfloat16 [1536, 6144], P(('dp', 'col'), 'row'), may hold values from -125 to 125
- grad_output: bfloat16 [1536, 6144], P(('dp', 'col'), 'row'), may hold values from -6 to 6
- pre_activation: bfloat16 [1536, 24576], P(('dp', 'row'), 'col'), may hold values from -6 to 6
- norm_gain_vector: float32 [6144], P('row'), may hold values from 0.5 to 1.5
- up_weight: bfloat16 [6144, 24576], P('row', 'col'), may hold values from -0.078125 to 0.078125
- down_weight: bfloat16 [24576, 6144], P('col', 'row'), may hold values from -0.0390625 to 0.0390625
Outputs:
- input_gradient: float32 [1536, 6144], P(('dp', 'col'), 'row')
- grad_up: float32 [6144, 24576], P(('row', 'dp'), 'col')
- grad_down: float32 [24576, 6144], P('col', ('row', 'dp'))
- grad_bias: float32 [24576], P('col')
- gain_gradient: float32 [6144], P('row')
The draws below stay inside these ranges and needn't reach their ends.
All inputs are finite; a program needn't handle non-finite values.
Results may differ from the reference program's by a relative error of at most 0.0055.
Values may be sent and summed in bfloat16 or wider, within the bound.
A program may use at most 256 MiB of HBM per device.

```python
import math
import jax
import jax.numpy as jnp
from jax import lax

MODEL_WIDTH = 6144
FF = 24576
TOKENS = 1536


def draw_layer_input(key, part):
    key_base = jax.random.fold_in(key, 11)
    key_values, key_rows, key_cols = jax.random.split(key_base, 3)
    low = math.log(0.5)
    high = math.log(5.0)
    row_scale = jnp.exp(jax.random.uniform(key_rows, (TOKENS, 1), jnp.float32, low, high))
    col_scale = jnp.exp(jax.random.uniform(key_cols, (1, MODEL_WIDTH), jnp.float32, low, high))
    values = jnp.clip(jax.random.normal(key_values, (TOKENS, MODEL_WIDTH), jnp.float32), -5.0, 5.0)
    return (values * row_scale * col_scale).astype(jnp.bfloat16)


def shard_levels(rng, shape, pieces, low, high):
    def one(axis_at, parts):
        draws = jax.random.uniform(jax.random.fold_in(jax.random.fold_in(rng, 6), axis_at), (parts,), jnp.float32, low / len(pieces), high / len(pieces))
        return jnp.repeat(jnp.exp(draws), shape[axis_at] // parts).reshape((-1,) + (1,) * (len(shape) - axis_at - 1))

    gain = one(*pieces[0])
    for cut in pieces[1:]:
        gain = gain * one(*cut)
    return gain


def gaussian(key, dims, deviation, reach, pieces=(), held_as=jnp.bfloat16):
    values = jax.random.normal(key, dims, jnp.float32) * deviation
    if len(pieces) > 0:
        values = shard_levels(key, dims, pieces, -0.22, 0.18) * values
    return jnp.clip(values, min=-reach, max=reach).astype(held_as)


def setup_inputs(seed: int = 0) -> dict:
    streams_of = jax.random.split(jax.random.key(seed), 7)
    layer_input = draw_layer_input(jax.random.fold_in(streams_of[6], 71), 0)
    grad_output = gaussian(streams_of[1], (TOKENS, MODEL_WIDTH), 1.0, 6.0, ((0, 8), (1, 4)))
    pre_activation = gaussian(streams_of[2], (TOKENS, FF), 1.0, 6.0, ((0, 8), (1, 4)))
    norm_gain_vector = jnp.clip(1.0 + 0.1 * jax.random.normal(streams_of[3], (MODEL_WIDTH,), jnp.float32), 0.5, 1.5)
    up_weight = gaussian(streams_of[4], (MODEL_WIDTH, FF), MODEL_WIDTH ** -0.5, 0.078125, ((0, 4), (1, 4)))
    down_weight = gaussian(streams_of[5], (FF, MODEL_WIDTH), FF ** -0.5, 0.0390625, ((0, 4), (1, 4)))
    return dict(layer_input=layer_input, grad_output=grad_output, pre_activation=pre_activation, norm_gain_vector=norm_gain_vector, up_weight=up_weight, down_weight=down_weight)


epsilon = 1e-06

def gelu_parts(pre_float):
    normal_cdf = 0.5 * (1.0 + lax.erf(pre_float * 0.7071067811865476))
    normal_pdf = jnp.exp(-0.5 * pre_float * pre_float) * 0.3989422804014327
    return (pre_float * normal_cdf, normal_cdf + pre_float * normal_pdf)

def reference(layer_input, grad_output, pre_activation, norm_gain_vector, up_weight, down_weight):
    input_single_precision = layer_input.astype(jnp.float32)
    row_average = lax.optimization_barrier(jnp.sum(input_single_precision, axis=1)) / MODEL_WIDTH
    square_rows = lax.optimization_barrier(jnp.sum(input_single_precision * input_single_precision, axis=1)) / MODEL_WIDTH
    reciprocal_deviation = 1.0 / jnp.sqrt(square_rows - row_average * row_average + epsilon)
    centered_standardized = (input_single_precision - row_average[:, None]) * reciprocal_deviation[:, None]
    normalized_rows = (centered_standardized * norm_gain_vector[None, :]).astype(jnp.bfloat16)
    gelu_value, gelu_slope = gelu_parts(pre_activation.astype(jnp.float32))
    activation = gelu_value.astype(jnp.bfloat16)
    grad_act = jnp.dot(grad_output, down_weight.T, preferred_element_type=jnp.float32)
    grad_hidden = (grad_act * gelu_slope).astype(jnp.bfloat16)
    normalized_gradient = jnp.dot(grad_hidden, up_weight.T, preferred_element_type=jnp.float32)
    grad_up = jnp.dot(normalized_rows.T, grad_hidden, preferred_element_type=jnp.float32)
    grad_down = jnp.dot(activation.T, grad_output, preferred_element_type=jnp.float32)
    grad_bias = lax.optimization_barrier(jnp.sum(grad_hidden.astype(jnp.float32), axis=0))
    gain_gradient = lax.optimization_barrier(jnp.sum(normalized_gradient * centered_standardized, axis=0))
    gain_scaled_rows = normalized_gradient * norm_gain_vector[None, :]
    leading_average = lax.optimization_barrier(jnp.sum(gain_scaled_rows, axis=1)) / MODEL_WIDTH
    trailing_average = lax.optimization_barrier(jnp.sum(gain_scaled_rows * centered_standardized, axis=1)) / MODEL_WIDTH
    input_gradient = reciprocal_deviation[:, None] * (gain_scaled_rows - leading_average[:, None] - centered_standardized * trailing_average[:, None])
    return (input_gradient, grad_up, grad_down, grad_bias, gain_gradient)
```

```python
import jax
import jax.numpy as jnp
from jax import lax
from jax.sharding import PartitionSpec as P

CHUNKS = 4
epsilon = 1e-06


def gelu_parts(pre_float):
    normal_cdf = 0.5 * (1.0 + lax.erf(pre_float * 0.7071067811865476))
    normal_pdf = jnp.exp(-0.5 * pre_float * pre_float) * 0.3989422804014327
    return (pre_float * normal_cdf, normal_cdf + pre_float * normal_pdf)


def contract_last(left, right):
    return lax.dot_general(
        left, right, (((1,), (1,)), ((), ())), preferred_element_type=jnp.float32
    )


def contract_first(left, right):
    return lax.dot_general(
        left, right, (((0,), (0,)), ((), ())), preferred_element_type=jnp.float32
    )


def build(sizes):
    swap = [(0, 1), (1, 0)]
    two = sizes["dp"] == 2

    def per_device(
        layer_input, grad_output, pre_activation, norm_gain_vector, up_weight, down_weight
    ):
        model_width = layer_input.shape[1] * sizes["row"]
        hidden = pre_activation.shape[1]
        chunks = CHUNKS if hidden % (CHUNKS * 128) == 0 else 1
        step = hidden // chunks
        me = lax.axis_index("dp")
        grad_all = lax.all_gather(grad_output, "col", axis=0, tiled=True)
        x = layer_input.astype(jnp.float32)
        sum_rows, square_rows = lax.psum(
            (jnp.sum(x, axis=1), jnp.sum(x * x, axis=1)), "row"
        )
        mean = sum_rows / model_width
        inv_std = 1.0 / jnp.sqrt(square_rows / model_width - mean * mean + epsilon)
        xhat = (x - mean[:, None]) * inv_std[:, None]
        normed = (xhat * norm_gain_vector[None, :]).astype(jnp.bfloat16)
        normed_all = lax.all_gather(normed, "col", axis=0, tiled=True)

        half = layer_input.shape[1] // sizes["dp"]

        def part(array, index):
            return lax.dynamic_slice_in_dim(array, index * half, half, axis=1)

        if two:
            normed_mine, normed_other = part(normed_all, me), part(normed_all, 1 - me)
            grad_mine, grad_other = part(grad_all, me), part(grad_all, 1 - me)

        def up_of(hid):
            if not two:
                return lax.psum_scatter(
                    contract_first(normed_all, hid), "dp", scatter_dimension=0, tiled=True
                )
            away = contract_first(normed_other, hid).astype(jnp.bfloat16)
            got = lax.ppermute(away, "dp", swap)
            return contract_first(normed_mine, hid) + got.astype(jnp.float32)

        def down_of(act):
            if not two:
                return lax.psum_scatter(
                    contract_first(act, grad_all), "dp", scatter_dimension=1, tiled=True
                )
            away = contract_first(act, grad_other).astype(jnp.bfloat16)
            got = lax.ppermute(away, "dp", swap)
            return contract_first(act, grad_mine) + got.astype(jnp.float32)

        ups, downs, biases, total = [], [], [], None
        for k in range(chunks):
            cut = slice(k * step, (k + 1) * step)
            value, slope = gelu_parts(pre_activation[:, cut].astype(jnp.float32))
            grad_act = lax.psum_scatter(
                contract_last(grad_all, down_weight[cut]).astype(jnp.bfloat16),
                "row",
                scatter_dimension=0,
                tiled=True,
            )
            act_all = lax.all_gather(value.astype(jnp.bfloat16), "row", axis=0, tiled=True)
            grad_hidden = (grad_act.astype(jnp.float32) * slope).astype(jnp.bfloat16)
            hid_all = lax.all_gather(grad_hidden, "row", axis=0, tiled=True)
            downs.append(down_of(act_all))
            ups.append(up_of(hid_all))
            biases.append(jnp.sum(hid_all.astype(jnp.float32), axis=0))
            term = contract_last(hid_all, up_weight[:, cut])
            total = term if total is None else total + term
        bias = jnp.concatenate(biases)
        grad_bias = bias + lax.ppermute(bias, "dp", swap) if two else lax.psum(bias, "dp")
        grad_up = jnp.concatenate(ups, axis=1)
        grad_down = jnp.concatenate(downs, axis=0)

        grad_normed = lax.psum_scatter(
            total.astype(jnp.bfloat16), "col", scatter_dimension=0, tiled=True
        ).astype(jnp.float32)
        scaled = grad_normed * norm_gain_vector[None, :]
        first, second = lax.psum(
            (jnp.sum(scaled, axis=1), jnp.sum(scaled * xhat, axis=1)), "row"
        )
        input_gradient = inv_std[:, None] * (
            scaled - first[:, None] / model_width - xhat * (second[:, None] / model_width)
        )
        gain_gradient = lax.psum(jnp.sum(grad_normed * xhat, axis=0), ("dp", "col"))
        return (input_gradient, grad_up, grad_down, grad_bias, gain_gradient)

    return per_device


def solution(mesh):
    placed = (
        P(("dp", "col"), "row"),
        P(("dp", "col"), "row"),
        P(("dp", "row"), "col"),
        P("row"),
        P("row", "col"),
        P("col", "row"),
    )
    return jax.shard_map(
        build(dict(mesh.shape)),
        mesh=mesh,
        in_specs=placed,
        out_specs=(
            P(("dp", "col"), "row"),
            P(("row", "dp"), "col"),
            P("col", ("row", "dp")),
            P("col"),
            P("row"),
        ),
        check_vma=False,
    )
```

```python
import jax
import jax.numpy as jnp
from jax import lax
from jax.sharding import PartitionSpec as P

CHUNKS = 4
epsilon = 1e-06


def gelu_parts(pre_float):
    normal_cdf = 0.5 * (1.0 + lax.erf(pre_float * 0.7071067811865476))
    normal_pdf = jnp.exp(-0.5 * pre_float * pre_float) * 0.3989422804014327
    return (pre_float * normal_cdf, normal_cdf + pre_float * normal_pdf)


def contract_last(left, right):
    return lax.dot_general(
        left, right, (((1,), (1,)), ((), ())), preferred_element_type=jnp.float32
    )


def contract_first(left, right):
    return lax.dot_general(
        left, right, (((0,), (0,)), ((), ())), preferred_element_type=jnp.float32
    )


def after(value, *others):
    return lax.optimization_barrier((value,) + others)[0]


def build(sizes):
    swap = [(0, 1), (1, 0)]
    two = sizes["dp"] == 2

    def body(
        layer_input, grad_output, pre_activation, norm_gain_vector, up_weight, down_weight
    ):
        model_width = layer_input.shape[1] * sizes["row"]
        hidden = pre_activation.shape[1]
        chunks = CHUNKS if hidden % (CHUNKS * 128) == 0 else 1
        step = hidden // chunks
        me = lax.axis_index("dp")
        grad_all = lax.all_gather(grad_output, "col", axis=0, tiled=True)
        x = layer_input.astype(jnp.float32)
        sum_rows, square_rows = lax.psum(
            (jnp.sum(x, axis=1), jnp.sum(x * x, axis=1)), "row"
        )
        mean = sum_rows / model_width
        inv_std = 1.0 / jnp.sqrt(square_rows / model_width - mean * mean + epsilon)
        xhat = (x - mean[:, None]) * inv_std[:, None]
        normed = (xhat * norm_gain_vector[None, :]).astype(jnp.bfloat16)
        normed_all = lax.all_gather(normed, "col", axis=0, tiled=True)

        half = layer_input.shape[1] // sizes["dp"]

        def part(array, index):
            return lax.dynamic_slice_in_dim(array, index * half, half, axis=1)

        if two:
            normed_mine, normed_other = part(normed_all, me), part(normed_all, 1 - me)
            grad_mine, grad_other = part(grad_all, me), part(grad_all, 1 - me)

        def away_up(hid):
            return contract_first(normed_other, hid).astype(jnp.bfloat16)

        def away_down(act):
            return contract_first(act, grad_other).astype(jnp.bfloat16)

        def finish_up(hid, got):
            if not two:
                return lax.psum_scatter(
                    contract_first(normed_all, hid), "dp", scatter_dimension=0, tiled=True
                )
            return contract_first(normed_mine, hid) + got.astype(jnp.float32)

        def finish_down(act, got):
            if not two:
                return lax.psum_scatter(
                    contract_first(act, grad_all), "dp", scatter_dimension=1, tiled=True
                )
            return contract_first(act, grad_mine) + got.astype(jnp.float32)

        def cut(k):
            return slice(k * step, (k + 1) * step)

        done = [grad_all, normed_all]
        extra = []

        def ordered(value):
            value = after(value, done[-2], *extra)
            extra.clear()
            return value

        def gather(value):
            out = lax.all_gather(ordered(value), "row", axis=0, tiled=True)
            done.append(out)
            return out

        def row_sum(k):
            out = lax.psum_scatter(
                ordered(contract_last(grad_all, down_weight[cut(k)]).astype(jnp.bfloat16)),
                "row",
                scatter_dimension=0,
                tiled=True,
            )
            done.append(out)
            return out

        activation = lax.optimization_barrier(
            gelu_parts(pre_activation.astype(jnp.float32))[0].astype(jnp.bfloat16)
        )
        grad_up = jnp.zeros((half, hidden), jnp.float32)
        grad_down = jnp.zeros((hidden, half), jnp.float32)
        biases, total = [], None
        held_down, held_up = [], []

        def send_down(k, act):
            got = None
            if two:
                away = away_down(act)
                got = lax.ppermute(away, "dp", swap)
                extra.append(away)
            held_down.append((k, act, got))

        act_all = gather(activation[:, cut(0)])
        sums = row_sum(0)
        send_down(0, act_all)
        for k in range(chunks):
            if k + 1 < chunks:
                act_all = gather(activation[:, cut(k + 1)])
            pre, sums = lax.optimization_barrier((pre_activation[:, cut(k)], sums))
            slope = gelu_parts(pre.astype(jnp.float32))[1]
            grad_hidden = (sums.astype(jnp.float32) * slope).astype(jnp.bfloat16)
            if len(held_up) > 1:
                at, *parts = held_up.pop(0)
                grad_up = lax.dynamic_update_slice(grad_up, finish_up(*parts), (0, at * step))
                extra.append(grad_up)
            hid_all = gather(grad_hidden)
            if k + 1 < chunks:
                send_down(k + 1, act_all)
                sums = row_sum(k + 1)
            got = None
            if two:
                away = away_up(hid_all)
                got = lax.ppermute(away, "dp", swap)
                extra.append(away)
            held_up.append((k, hid_all, got))
            biases.append(jnp.sum(hid_all.astype(jnp.float32), axis=0))
            term = contract_last(hid_all, up_weight[:, cut(k)])
            total = term if total is None else total + term
            if len(held_down) > 2:
                at, *parts = held_down.pop(0)
                grad_down = lax.dynamic_update_slice(
                    grad_down, finish_down(*parts), (at * step, 0)
                )
                extra.append(grad_down)
            extra.append(total)
        extra.clear()
        bias = jnp.concatenate(biases)
        grad_bias = bias + lax.ppermute(bias, "dp", swap) if two else lax.psum(bias, "dp")
        grad_normed = lax.psum_scatter(total, "col", scatter_dimension=0, tiled=True)
        for at, *parts in held_down:
            grad_down = lax.dynamic_update_slice(grad_down, finish_down(*parts), (at * step, 0))
        for at, *parts in held_up:
            grad_up = lax.dynamic_update_slice(grad_up, finish_up(*parts), (0, at * step))
        scaled = grad_normed * norm_gain_vector[None, :]
        first, second = lax.psum(
            (jnp.sum(scaled, axis=1), jnp.sum(scaled * xhat, axis=1)), "row"
        )
        input_gradient = inv_std[:, None] * (
            scaled - first[:, None] / model_width - xhat * (second[:, None] / model_width)
        )
        gain_gradient = lax.psum(jnp.sum(grad_normed * xhat, axis=0), ("dp", "col"))
        return (input_gradient, grad_up, grad_down, grad_bias, gain_gradient)

    return body


def solution(mesh):
    placed = (
        P(("dp", "col"), "row"),
        P(("dp", "col"), "row"),
        P(("dp", "row"), "col"),
        P("row"),
        P("row", "col"),
        P("col", "row"),
    )
    return jax.shard_map(
        build(dict(mesh.shape)),
        mesh=mesh,
        in_specs=placed,
        out_specs=(
            P(("dp", "col"), "row"),
            P(("row", "dp"), "col"),
            P("col", ("row", "dp")),
            P("col"),
            P("row"),
        ),
        check_vma=False,
    )
```
